128 devices in a mesh: outer: 8 (over x, z_lo), inner: 16 (over z_hi, y, core).
Axes of the slice: x: 4, y: 4, z: 4 (z_hi: 2, z_lo: 2; z = z_hi * 2 + z_lo), core: 2. Of those that a mesh axis runs over, the one named last changes fastest.
Arguments:
- gate_in: bfloat16 [16384, 4096], P(('outer', 'inner')), may hold values from -6 to 6
- value_in: bfloat16 [16384, 4096], P(('outer', 'inner')), may hold values from -6 to 6
- gate_out: bfloat16 [16384, 4096], P(('outer', 'inner')), may hold values from -6 to 6
- filters: bfloat16 [16384, 4096], P(('outer', 'inner')), may hold values from -1.04 to 1.04
- skip_bias: float32 [4096], replicated, may hold values from 0.5 to 1.5
Outputs:
- mixer_out: bfloat16 [16384, 4096], P(('outer', 'inner'))
The draws below stay inside these ranges and needn't reach their ends.
All inputs are finite; a program needn't handle non-finite values.
Results may differ from the reference program's by a relative error of at most 0.009.
Values may be sent and summed in bfloat16 or wider, within the bound.
A program may use at most 128 MiB of HBM per device.

```python
import math
import jax
import jax.numpy as jnp
from jax import lax

CHANNEL_SHARE = 4096
TOKEN_COUNT = 16384


def draw_filters(key, part):
    key_lasting = jax.random.fold_in(key, 11)
    key_rough = jax.random.fold_in(key, 12)
    key_slow = jax.random.fold_in(key, 13)
    key_fast = jax.random.fold_in(key, 14)
    spike_key = jax.random.fold_in(key, 15)
    dropout_key = jax.random.fold_in(key, 16)
    token_places = jnp.arange(TOKEN_COUNT, dtype=jnp.float32)[:, None]
    lasting = jax.random.bernoulli(key_lasting, 0.5, (CHANNEL_SHARE,))
    roughness = jnp.clip(jax.random.normal(key_rough, (TOKEN_COUNT, CHANNEL_SHARE), jnp.float32), -4.0, 4.0)
    slow_rate = jnp.exp(jax.random.uniform(key_slow, (CHANNEL_SHARE,), jnp.float32, math.log(0.3), math.log(2.0))) / TOKEN_COUNT
    fast_rate = jnp.exp(jax.random.uniform(key_fast, (CHANNEL_SHARE,), jnp.float32, math.log(1.0 / 50.0), math.log(1.0 / 30.0)))
    decay_rate = jnp.where(lasting, slow_rate, fast_rate)
    decay_profile = jnp.sqrt(2.0 * decay_rate)[None, :] * jnp.exp(-decay_rate[None, :] * token_places)
    far_tail = jnp.where(token_places >= 64.0, 0.02 * jnp.exp(-slow_rate[None, :] * token_places), 0.0)
    decay_profile = decay_profile + jnp.where(lasting[None, :], 0.0, far_tail)
    spike_events = jax.random.randint(spike_key, (4, CHANNEL_SHARE), 1, TOKEN_COUNT)
    spike_dropout = jax.random.uniform(dropout_key, (4, CHANNEL_SHARE), jnp.float32, 0.5, 0.8)
    for token_index in range(4):
        decay_profile = decay_profile * jnp.where(token_places >= spike_events[token_index].astype(jnp.float32)[None, :], spike_dropout[token_index][None, :], 1.0)
    return (decay_profile * roughness).astype(jnp.bfloat16)


def block_scale(rng, shape, cuts, smallest, largest):
    gain, own = 1.0, jax.random.fold_in(rng, 6)
    for position, shards_of in cuts:
        draws = jnp.exp(jax.random.uniform(jax.random.fold_in(own, position), (shards_of,), jnp.float32, smallest / len(cuts), largest / len(cuts)))
        gain = gain * jnp.repeat(draws, shape[position] // shards_of).reshape([-1 if axis == position else 1 for axis in range(len(shape))])
    return gain


def scatter_about(stream_key, extent, width, reach, shards=(), held_as=jnp.bfloat16):
    drawn = width * jax.random.normal(stream_key, extent, jnp.float32)
    if shards:
        drawn = drawn * block_scale(stream_key, extent, shards, -0.22, 0.18)
    return jnp.clip(drawn, -reach, reach).astype(held_as)


def setup_inputs(seed: int = 0) -> dict:
    seeds = jax.random.split(jax.random.key(seed), 6)
    gate_in = scatter_about(seeds[0], (TOKEN_COUNT, CHANNEL_SHARE), 1.0, 6.0, ((0, 128),))
    value_in = scatter_about(seeds[1], (TOKEN_COUNT, CHANNEL_SHARE), 1.0, 6.0, ((0, 128),))
    gate_out = scatter_about(seeds[2], (TOKEN_COUNT, CHANNEL_SHARE), 1.0, 6.0, ((0, 128),))
    filters = draw_filters(jax.random.fold_in(seeds[5], 71), 0)
    skip_bias = jnp.clip(jax.random.uniform(seeds[4], (CHANNEL_SHARE,), jnp.float32, 0.5, 1.5), 0.5, 1.5)
    return dict(gate_in=gate_in, value_in=value_in, gate_out=gate_out, filters=filters, skip_bias=skip_bias)


def causal_block(signal, response):
    padded = 2 * signal.shape[0]
    left_side = jnp.fft.rfft(signal, n=padded, axis=0)
    right_side = jnp.fft.rfft(response, n=padded, axis=0)
    return jnp.fft.irfft(left_side * right_side, n=padded, axis=0)[: signal.shape[0]]


def reference(gate_in, value_in, gate_out, filters, skip_bias):
    modulated = (gate_in.astype(jnp.float32) * value_in.astype(jnp.float32)).astype(jnp.bfloat16)
    signal = modulated.astype(jnp.float32)
    response = filters.astype(jnp.float32)
    blocks = CHANNEL_SHARE // 16
    signal_blocks = signal.reshape(TOKEN_COUNT, blocks, 16).transpose(1, 0, 2)
    response_blocks = response.reshape(TOKEN_COUNT, blocks, 16).transpose(1, 0, 2)
    convolved = lax.map(lambda couple: causal_block(couple[0], couple[1]), (signal_blocks, response_blocks))
    convolved = convolved.transpose(1, 0, 2).reshape(TOKEN_COUNT, CHANNEL_SHARE)
    result = gate_out.astype(jnp.float32) * (convolved + skip_bias.astype(jnp.float32)[None, :] * signal)
    return result.astype(jnp.bfloat16)
```

```python
import functools
import math

import jax
import jax.numpy as jnp
import numpy as np
from jax import lax
from jax.experimental import pallas as pl
from jax.experimental.pallas import tpu as pltpu
from jax.sharding import PartitionSpec as P

MESH = pl.DeviceIdType.MESH
DEVICES = 128
BLOCK = 128
CHUNKS = 2
SHARE = 16
GROUPS = 16
MEMBERS = 8
BF, F32 = jnp.bfloat16, jnp.float32


def tables():
    total = DEVICES * BLOCK
    place = np.arange(128)
    shifted = place + 0.25
    phi = 2.0 * math.pi * np.outer(shifted, place) / 128
    tau = 2.0 * math.pi * np.outer(shifted, place) / total
    psi = 2.0 * math.pi * np.outer(place, place) / 128
    c, s = np.cos(psi), np.sin(psi)
    first = np.concatenate([np.cos(phi), -np.sin(phi)], 0)
    second = np.block([[c, -s], [s, c]])
    second_back = np.block([[c, s], [-s, c]])
    first_back = np.concatenate([np.cos(phi).T, -np.sin(phi).T], 1) / total
    return (
        jnp.asarray(first, BF),
        jnp.asarray(np.cos(tau), F32),
        jnp.asarray(-np.sin(tau), F32),
        jnp.asarray(second, BF),
        jnp.asarray(second_back, BF),
        jnp.asarray(first_back, BF),
    )


def dot(a, b):
    return jnp.dot(a, b, preferred_element_type=F32)


def kernel(
    gate_hbm, value_hbm, gout_hbm, filt_hbm, skip_ref, f1, tr_ref, ti_ref, f2, f2b, f1b, out_hbm,
    gate, value, gout, filt, outv, send, recv, wide, owide, osend, orecv,
    load_sem, store_sem, self_sem, in_send, in_recv, out_send, out_recv,
):
    half = GROUPS * 128
    outer, inner = lax.axis_index("outer"), lax.axis_index("inner")
    me = outer * 16 + inner
    x0, z0 = outer // 2, lax.rem(outer, 2) + 2 * (inner // 8)
    y0, c0 = lax.rem(inner // 2, 4), lax.rem(inner, 2)
    u0, v0 = lax.rem(y0 + 4 - x0, 4), lax.rem(z0 + 4 - x0, 4)
    my_group, my_member = u0 * 4 + v0, x0 * 2 + c0

    barrier = pltpu.get_barrier_semaphore()

    def greet(i, carry):
        d = lax.rem(me + i, DEVICES)
        pl.semaphore_signal(barrier, inc=1, device_id=(d // 16, lax.rem(d, 16)), device_id_type=MESH)
        return carry

    loads = []
    for k in range(CHUNKS):
        lanes = pl.ds(k * half, half)
        loads.append([
            pltpu.make_async_copy(src.at[:, lanes], dst.at[:, lanes], load_sem.at[k, n])
            for n, (src, dst) in enumerate([(gate_hbm, gate), (value_hbm, value), (filt_hbm, filt)])
        ])
        for copy in loads[k]:
            copy.start()
    gout_load = pltpu.make_async_copy(gout_hbm, gout, load_sem.at[0, 3])
    gout_load.start()
    lax.fori_loop(1, DEVICES, greet, 0)

    def group_at(step):
        u, v = lax.rem(u0 + step // 4, 4), lax.rem(v0 + step, 4)
        return u, v, u * 4 + v

    def partner(u, v, n):
        x, c = lax.rem(x0 + n // 2, 4), lax.rem(c0 + n, 2)
        y, z = lax.rem(x + u, 4), lax.rem(x + v, 4)
        return (x * 2 + lax.rem(z, 2), (z // 2) * 8 + y * 2 + c), x * 2 + c

    def prepare(k, step):
        _, _, g = group_at(step)
        lanes = pl.ds(pl.multiple_of(k * half + g * 128, 128), 128)
        signal = (gate[:, lanes].astype(F32) * value[:, lanes].astype(F32)).astype(BF)
        send[k, g, :, 0] = signal.T.reshape(MEMBERS, SHARE, BLOCK)
        send[k, g, :, 1] = filt[:, lanes].T.reshape(MEMBERS, SHARE, BLOCK)

    def ship_in(k, step, first):
        u, v, g = group_at(step)
        for n in range(first, MEMBERS):
            where, m = partner(u, v, n)
            pltpu.make_async_remote_copy(
                src_ref=send.at[k, g, m], dst_ref=recv.at[k, me], send_sem=in_send.at[k],
                recv_sem=in_recv.at[k], device_id=where, device_id_type=MESH,
            ).start()

    def ship_out(k, step, first):
        u, v, _ = group_at(step)
        for n in range(first, MEMBERS):
            where, _ = partner(u, v, n)
            pltpu.make_async_remote_copy(
                src_ref=osend.at[k, where[0] * 16 + where[1]], dst_ref=orecv.at[k, my_group, my_member],
                send_sem=out_send.at[k], recv_sem=out_recv.at[k], device_id=where, device_id_type=MESH,
            ).start()

    def all_in(k):
        part = pl.ds(0, DEVICES - 1)
        return pltpu.make_async_remote_copy(
            src_ref=recv.at[k, part], dst_ref=recv.at[k, part], send_sem=in_send.at[k], recv_sem=in_recv.at[k],
            device_id=(outer, inner), device_id_type=MESH,
        )

    def all_out(k):
        part = pl.ds(0, DEVICES - 1)
        return pltpu.make_async_remote_copy(
            src_ref=osend.at[k, part], dst_ref=osend.at[k, part], send_sem=out_send.at[k],
            recv_sem=out_recv.at[k], device_id=(outer, inner), device_id_type=MESH,
        )

    def loop(start, stop, body, unroll=1):
        def step(i, carry):
            body(i)
            return carry

        lax.fori_loop(start, stop, step, 0, unroll=unroll)

    def convolve(k):
        def widen(i):
            rows = pl.ds(pl.multiple_of(i * 256, 256), 256)
            wide[rows, :] = recv[k, pl.ds(i * 8, 8)].astype(F32).reshape(256, BLOCK)

        loop(0, DEVICES // 8, widen, unroll=2)

        def channel(i):
            pair = [
                wide[pl.ds(arr * SHARE + i * 2 + e, DEVICES, stride=2 * SHARE), :].astype(BF)
                for e in range(2)
                for arr in range(2)
            ]
            spread = dot(f1[...], jnp.concatenate(pair, axis=1))
            tr, ti = tr_ref[...], ti_ref[...]
            rows = []
            for n in range(4):
                re, im = spread[:128, n * 128 : n * 128 + 128], spread[128:, n * 128 : n * 128 + 128]
                rows.append(jnp.concatenate([re * tr - im * ti, re * ti + im * tr], axis=1).astype(BF))
            spectra = dot(jnp.concatenate(rows, axis=0), f2[...])
            rows = []
            for e in range(2):
                sig, res = spectra[e * 256 : e * 256 + 128], spectra[e * 256 + 128 : e * 256 + 256]
                sr, si, hr, hi = sig[:, :128], sig[:, 128:], res[:, :128], res[:, 128:]
                rows.append(jnp.concatenate([sr * hr - si * hi, sr * hi + si * hr], axis=1).astype(BF))
            back = dot(jnp.concatenate(rows, axis=0), f2b[...])
            columns = []
            for e in range(2):
                re, im = back[e * 128 : e * 128 + 128, :128], back[e * 128 : e * 128 + 128, 128:]
                columns.append(jnp.concatenate([re * tr + im * ti, im * tr - re * ti], axis=0).astype(BF))
            result = dot(f1b[...], jnp.concatenate(columns, axis=1))
            for e in range(2):
                owide[pl.ds(i * 2 + e, DEVICES, stride=SHARE), :] = result[:, e * 128 : e * 128 + 128]

        loop(0, SHARE // 2, channel)

        def narrow(i):
            rows = pl.ds(pl.multiple_of(i * 256, 256), 256)
            osend[k, pl.ds(i * 16, 16)] = owide[rows, :].reshape(16, SHARE, BLOCK).astype(BF)

        loop(0, DEVICES // 16, narrow, unroll=2)

    def finish(k, g):
        lanes = pl.ds(pl.multiple_of(k * half + g * 128, 128), 128)
        convolved = orecv[k, g].reshape(128, BLOCK).T.astype(F32)
        signal = (gate[:, lanes].astype(F32) * value[:, lanes].astype(F32)).astype(BF).astype(F32)
        result = gout[:, lanes].astype(F32) * (convolved + skip_ref[:, lanes] * signal)
        outv[:, lanes] = result.astype(BF)

    own_in = [
        pltpu.make_async_copy(send.at[k, my_group, my_member], recv.at[k, me], self_sem.at[0, k])
        for k in range(CHUNKS)
    ]
    own_out = [
        pltpu.make_async_copy(osend.at[k, me], orecv.at[k, my_group, my_member], self_sem.at[1, k])
        for k in range(CHUNKS)
    ]
    for k in range(CHUNKS):
        for copy in loads[k]:
            copy.wait()
        loop(0, GROUPS, functools.partial(prepare, k), unroll=2)
        if k == 0:
            pl.semaphore_wait(barrier, DEVICES - 1)
        ship_in(k, 0, 1)
        loop(1, GROUPS, lambda step: ship_in(k, step, 0))
        own_in[k].start()
    for k in range(CHUNKS):
        all_in(k).wait_recv()
        own_in[k].wait()
        convolve(k)
        ship_out(k, 0, 1)
        loop(1, GROUPS, lambda step: ship_out(k, step, 0))
        own_out[k].start()
    gout_load.wait()
    stores = []
    for k in range(CHUNKS):
        all_out(k).wait_recv()
        own_out[k].wait()
        loop(0, GROUPS, functools.partial(finish, k), unroll=2)
        lanes = pl.ds(k * half, half)
        stores.append(pltpu.make_async_copy(outv.at[:, lanes], out_hbm.at[:, lanes], store_sem.at[k]))
        stores[k].start()
    for k in range(CHUNKS):
        all_in(k).wait_send()
        all_out(k).wait_send()
        stores[k].wait()


def shards(gate_in, value_in, gate_out, filters, skip_bias):
    rows, channels = gate_in.shape
    any_spec = pl.BlockSpec(memory_space=pl.ANY)
    vmem_spec = pl.BlockSpec(memory_space=pltpu.VMEM)
    full = pltpu.VMEM((rows, channels), BF)
    dma = pltpu.SemaphoreType.DMA
    return pl.pallas_call(
        kernel,
        out_shape=jax.ShapeDtypeStruct((rows, channels), BF),
        in_specs=[any_spec] * 4 + [vmem_spec] * 7,
        out_specs=any_spec,
        scratch_shapes=[
            full, full, full, full, full,
            pltpu.VMEM((CHUNKS, GROUPS, MEMBERS, 2, SHARE, BLOCK), BF),
            pltpu.VMEM((CHUNKS, DEVICES, 2, SHARE, BLOCK), BF),
            pltpu.VMEM((DEVICES * 2 * SHARE, BLOCK), F32),
            pltpu.VMEM((DEVICES * SHARE, BLOCK), F32),
            pltpu.VMEM((CHUNKS, DEVICES, SHARE, BLOCK), BF),
            pltpu.VMEM((CHUNKS, GROUPS, MEMBERS, SHARE, BLOCK), BF),
            dma((CHUNKS, 4)), dma((CHUNKS,)), dma((2, CHUNKS)),
            dma((CHUNKS,)), dma((CHUNKS,)), dma((CHUNKS,)), dma((CHUNKS,)),
        ],
        compiler_params=pltpu.CompilerParams(collective_id=0, has_side_effects=True, vmem_limit_bytes=40 * 2**20),
        name="gated_convolution",
    )(gate_in, value_in, gate_out, filters, skip_bias.reshape(1, channels), *tables())


def solution(mesh):
    spread = P(("outer", "inner"), None)
    return jax.shard_map(
        shards, mesh=mesh, in_specs=(spread,) * 4 + (P(),), out_specs=spread, check_vma=False
    )
```

```python
import functools
import math

import jax
import jax.numpy as jnp
import numpy as np
from jax import lax
from jax.experimental import pallas as pl
from jax.experimental.pallas import tpu as pltpu
from jax.sharding import PartitionSpec as P

MESH = pl.DeviceIdType.MESH
DEVICES = 128
BLOCK = 128
CHUNKS = 2
SHARE = 16
GROUPS = 16
MEMBERS = 8
BF, F32 = jnp.bfloat16, jnp.float32


def tables():
    total = DEVICES * BLOCK
    place = np.arange(128)
    shifted = place + 0.25
    phi = 2.0 * math.pi * np.outer(shifted, place) / 128
    tau = 2.0 * math.pi * np.outer(shifted, place) / total
    psi = 2.0 * math.pi * np.outer(place, place) / 128
    c, s = np.cos(psi), np.sin(psi)
    first = np.concatenate([np.cos(phi), -np.sin(phi)], 0)
    second = np.block([[c, -s], [s, c]])
    second_back = np.block([[c, s], [-s, c]])
    first_back = np.concatenate([np.cos(phi).T, -np.sin(phi).T], 1) / total
    square = np.concatenate([second, second_back, first_back, np.pad(first, ((0, 0), (0, 128)))], 0)
    turn = np.stack([np.cos(tau), -np.sin(tau)])
    return jnp.asarray(square, BF), jnp.asarray(turn, F32)


def dot(a, b):
    return jnp.dot(a, b, preferred_element_type=F32)


def kernel(
    gate_hbm, value_hbm, gout_hbm, filt_hbm, skip_hbm, square_hbm, turn_hbm, out_hbm,
    gate, value, gout, filt, skip_ref, square, turn, outv, send, recv, wide, owide, turned, product, unturned, osend, orecv,
    load_sem, late_sem, store_sem, self_sem, in_send, in_recv, out_send, out_recv, core_sem, y_sem, z_sem,
):
    half = GROUPS * 128
    outer, inner = lax.axis_index("outer"), lax.axis_index("inner")
    me = outer * 16 + inner
    x0, z0 = outer // 2, lax.rem(outer, 2) + 2 * (inner // 8)
    y0, c0 = lax.rem(inner // 2, 4), lax.rem(inner, 2)
    u0, v0 = lax.rem(y0 + 4 - x0, 4), lax.rem(z0 + 4 - x0, 4)
    my_group, my_member = u0 * 4 + v0, x0 * 2 + c0

    barrier = pltpu.get_barrier_semaphore()

    def place(x, y, z, c):
        return x * 2 + lax.rem(z, 2), (z // 2) * 8 + y * 2 + c

    along_x = [place(lax.rem(x0 + n, 4), y0, z0, c0) for n in range(1, 4)]
    along_y = [place(x0, lax.rem(y0 + n, 4), z0, c0) for n in range(1, 4)]
    along_z = [place(x0, y0, lax.rem(z0 + n, 4), c0) for n in range(1, 4)]
    other_core = [place(x0, y0, z0, 1 - c0)]

    def greet(sem, devices):
        for where in devices:
            pl.semaphore_signal(sem, inc=1, device_id=where, device_id_type=MESH)

    greet(barrier, along_x + along_y + along_z + other_core)

    loads = []
    for k in range(CHUNKS):
        lanes = pl.ds(k * half, half)
        loads.append([
            pltpu.make_async_copy(src.at[:, lanes], dst.at[:, lanes], load_sem.at[k, n])
            for n, (src, dst) in enumerate([(gate_hbm, gate), (value_hbm, value), (filt_hbm, filt)])
        ])
        for copy in loads[k]:
            copy.start()
    late = [
        pltpu.make_async_copy(src, dst, late_sem.at[n])
        for n, (src, dst) in enumerate([
            (square_hbm, square), (turn_hbm, turn), (skip_hbm, skip_ref), (gout_hbm, gout)
        ])
    ]
    for copy in late:
        copy.start()

    def group_at(step):
        u, v = lax.rem(u0 + step // 4, 4), lax.rem(v0 + step, 4)
        return u, v, u * 4 + v

    def partner(u, v, n):
        x, c = lax.rem(x0 + n // 2, 4), lax.rem(c0 + n, 2)
        y, z = lax.rem(x + u, 4), lax.rem(x + v, 4)
        return (x * 2 + lax.rem(z, 2), (z // 2) * 8 + y * 2 + c), x * 2 + c

    def prepare(k, step):
        _, _, g = group_at(step)
        lanes = pl.ds(pl.multiple_of(k * half + g * 128, 128), 128)
        signal = (gate[:, lanes].astype(F32) * value[:, lanes].astype(F32)).astype(BF)
        send[k, g, :, 0] = signal.T.reshape(MEMBERS, SHARE, BLOCK)
        send[k, g, :, 1] = filt[:, lanes].T.reshape(MEMBERS, SHARE, BLOCK)

    def ship_in(k, step, first):
        u, v, g = group_at(step)
        for n in range(first, MEMBERS):
            where, m = partner(u, v, n)
            pltpu.make_async_remote_copy(
                src_ref=send.at[k, g, m], dst_ref=recv.at[k, me], send_sem=in_send.at[k],
                recv_sem=in_recv.at[k], device_id=where, device_id_type=MESH,
            ).start()

    def ship_out(k, step, first):
        u, v, _ = group_at(step)
        for n in range(first, MEMBERS):
            where, _ = partner(u, v, n)
            pltpu.make_async_remote_copy(
                src_ref=osend.at[k, where[0] * 16 + where[1]], dst_ref=orecv.at[k, my_group, my_member],
                send_sem=out_send.at[k], recv_sem=out_recv.at[k], device_id=where, device_id_type=MESH,
            ).start()

    def all_in(k):
        part = pl.ds(0, DEVICES - 1)
        return pltpu.make_async_remote_copy(
            src_ref=recv.at[k, part], dst_ref=recv.at[k, part], send_sem=in_send.at[k], recv_sem=in_recv.at[k],
            device_id=(outer, inner), device_id_type=MESH,
        )

    def all_out(k):
        part = pl.ds(0, DEVICES - 1)
        return pltpu.make_async_remote_copy(
            src_ref=osend.at[k, part], dst_ref=osend.at[k, part], send_sem=out_send.at[k],
            recv_sem=out_recv.at[k], device_id=(outer, inner), device_id_type=MESH,
        )

    def loop(start, stop, body, unroll=1):
        def step(i, carry):
            body(i)
            return carry

        lax.fori_loop(start, stop, step, 0, unroll=unroll)

    def convolve(k):
        def widen(i):
            rows = pl.ds(pl.multiple_of(i * 256, 256), 256)
            wide[rows, :] = recv[k, pl.ds(i * 8, 8)].astype(F32).reshape(256, BLOCK)

        loop(0, DEVICES // 8, widen, unroll=2)

        def stage_first(i):
            pair = [
                wide[pl.ds(arr * SHARE + i * 2 + e, DEVICES, stride=2 * SHARE), :].astype(BF)
                for e in range(2)
                for arr in range(2)
            ]
            spread = dot(square[640:896, :128], jnp.concatenate(pair, axis=1))
            tr, ti = turn[0], turn[1]
            for n in range(4):
                re, im = spread[:128, n * 128 : n * 128 + 128], spread[128:, n * 128 : n * 128 + 128]
                turned[n * 128 : n * 128 + 128, :128] = (re * tr - im * ti).astype(BF)
                turned[n * 128 : n * 128 + 128, 128:] = (re * ti + im * tr).astype(BF)

        def stage_product():
            spectra = dot(turned[...], square[0:256, :])
            for e in range(2):
                sig, res = spectra[e * 256 : e * 256 + 128], spectra[e * 256 + 128 : e * 256 + 256]
                sr, si, hr, hi = sig[:, :128], sig[:, 128:], res[:, :128], res[:, 128:]
                product[e * 128 : e * 128 + 128, :128] = (sr * hr - si * hi).astype(BF)
                product[e * 128 : e * 128 + 128, 128:] = (sr * hi + si * hr).astype(BF)

        def stage_back():
            back = dot(product[...], square[256:512, :])
            tr, ti = turn[0], turn[1]
            for e in range(2):
                re, im = back[e * 128 : e * 128 + 128, :128], back[e * 128 : e * 128 + 128, 128:]
                unturned[:128, e * 128 : e * 128 + 128] = (re * tr + im * ti).astype(BF)
                unturned[128:, e * 128 : e * 128 + 128] = (im * tr - re * ti).astype(BF)

        def stage_last(i):
            result = dot(square[512:640, :], unturned[...])
            for e in range(2):
                owide[pl.ds(i * 2 + e, DEVICES, stride=SHARE), :] = result[:, e * 128 : e * 128 + 128]

        pairs = SHARE // 2
        stage_first(0)
        stage_product()
        stage_first(1)
        stage_back()
        stage_product()
        stage_first(2)

        def steady(i):
            stage_last(i)
            stage_back()
            stage_product()
            stage_first(i + 3)

        loop(0, pairs - 3, steady)
        stage_last(pairs - 3)
        stage_back()
        stage_product()
        stage_last(pairs - 2)
        stage_back()
        stage_last(pairs - 1)

        def narrow(i):
            rows = pl.ds(pl.multiple_of(i * 256, 256), 256)
            osend[k, pl.ds(i * 16, 16)] = owide[rows, :].reshape(16, SHARE, BLOCK).astype(BF)

        loop(0, DEVICES // 16, narrow, unroll=2)

    def finish(k, g):
        lanes = pl.ds(pl.multiple_of(k * half + g * 128, 128), 128)
        convolved = orecv[k, g].reshape(128, BLOCK).T.astype(F32)
        signal = (gate[:, lanes].astype(F32) * value[:, lanes].astype(F32)).astype(BF).astype(F32)
        result = gout[:, lanes].astype(F32) * (convolved + skip_ref[:, lanes] * signal)
        outv[:, lanes] = result.astype(BF)

    own_in = [
        pltpu.make_async_copy(send.at[k, my_group, my_member], recv.at[k, me], self_sem.at[0, k])
        for k in range(CHUNKS)
    ]
    own_out = [
        pltpu.make_async_copy(osend.at[k, me], orecv.at[k, my_group, my_member], self_sem.at[1, k])
        for k in range(CHUNKS)
    ]
    for k in range(CHUNKS):
        for copy in loads[k]:
            copy.wait()
        loop(0, GROUPS, functools.partial(prepare, k), unroll=2)
        if k == 0:
            pl.semaphore_wait(barrier, 10)
            for sem, devices in ((core_sem, other_core), (y_sem, along_y), (z_sem, along_z)):
                greet(sem, devices)
                pl.semaphore_wait(sem, len(devices))
        ship_in(k, 0, 1)
        loop(1, GROUPS, lambda step: ship_in(k, step, 0))
        own_in[k].start()
    for copy in late:
        copy.wait()
    for k in range(CHUNKS):
        all_in(k).wait_recv()
        own_in[k].wait()
        convolve(k)
        if k + 1 < CHUNKS:
            all_in(k + 1).wait_send()
        ship_out(k, 0, 1)
        loop(1, GROUPS, lambda step: ship_out(k, step, 0))
        own_out[k].start()
    stores = []
    for k in range(CHUNKS):
        all_out(k).wait_recv()
        own_out[k].wait()
        loop(0, GROUPS, functools.partial(finish, k), unroll=2)
        lanes = pl.ds(k * half, half)
        stores.append(pltpu.make_async_copy(outv.at[:, lanes], out_hbm.at[:, lanes], store_sem.at[k]))
        stores[k].start()
    for k in range(CHUNKS):
        if k == 0:
            all_in(k).wait_send()
        all_out(k).wait_send()
        stores[k].wait()


def shards(gate_in, value_in, gate_out, filters, skip_bias):
    rows, channels = gate_in.shape
    any_spec = pl.BlockSpec(memory_space=pl.ANY)
    full = pltpu.VMEM((rows, channels), BF)
    dma, regular = pltpu.SemaphoreType.DMA, pltpu.SemaphoreType.REGULAR
    return pl.pallas_call(
        kernel,
        out_shape=jax.ShapeDtypeStruct((rows, channels), BF),
        in_specs=[any_spec] * 7,
        out_specs=any_spec,
        scratch_shapes=[
            full, full, full, full,
            pltpu.VMEM((1, channels), F32), pltpu.VMEM((896, 256), BF), pltpu.VMEM((2, 128, 128), F32),
            full,
            pltpu.VMEM((CHUNKS, GROUPS, MEMBERS, 2, SHARE, BLOCK), BF),
            pltpu.VMEM((CHUNKS, DEVICES, 2, SHARE, BLOCK), BF),
            pltpu.VMEM((DEVICES * 2 * SHARE, BLOCK), F32),
            pltpu.VMEM((DEVICES * SHARE, BLOCK), F32),
            pltpu.VMEM((512, 256), BF), pltpu.VMEM((256, 256), BF), pltpu.VMEM((256, 256), BF),
            pltpu.VMEM((CHUNKS, DEVICES, SHARE, BLOCK), BF),
            pltpu.VMEM((CHUNKS, GROUPS, MEMBERS, SHARE, BLOCK), BF),
            dma((CHUNKS, 3)), dma((4,)), dma((CHUNKS,)), dma((2, CHUNKS)),
            dma((CHUNKS,)), dma((CHUNKS,)), dma((CHUNKS,)), dma((CHUNKS,)),
            regular, regular, regular,
        ],
        compiler_params=pltpu.CompilerParams(collective_id=0, has_side_effects=True, vmem_limit_bytes=63 * 2**20),
        name="gated_convolution",
    )(gate_in, value_in, gate_out, filters, skip_bias.reshape(1, channels), *tables())


def solution(mesh):
    spread = P(("outer", "inner"), None)
    return jax.shard_map(
        shards, mesh=mesh, in_specs=(spread,) * 4 + (P(),), out_specs=spread, check_vma=False
    )
```
